512 devices in a mesh: dp: 4 (over y), ctx: 128 (over z, x, core).
Axes of the slice: x: 4, y: 4, z: 16, core: 2. Of those that a mesh axis runs over, the one named last changes fastest.
Arguments:
- queries: bfloat16 [147456, 2048], P(('dp', 'ctx')), may hold values from -6.5 to 6.5
- key_rows: bfloat16 [147456, 512], P(('dp', 'ctx')), may hold values from -6.5 to 6.5
- value_rows: bfloat16 [147456, 512], P(('dp', 'ctx')), may hold values from -6 to 6
- slab_row: int32 [147456], P(('dp', 'ctx')), may hold values from -1 to 131071, as said below
- doc_lengths: int32 [4, 96], P('dp'), may hold values from 1 to 512, 32768 in all within a row
- out_grad: bfloat16 [131072, 2048], P(('dp', 'ctx')), may hold values from -6 to 6
Outputs:
- grad_queries: bfloat16 [131072, 2048], P(('dp', 'ctx'))
- grad_keys: bfloat16 [131072, 512], P(('dp', 'ctx'))
- grad_values: bfloat16 [131072, 512], P(('dp', 'ctx'))
The draws below stay inside these ranges and needn't reach their ends.
Inputs may be any that keep to these rules, and one draw needn't show every extreme that they name: `slab_row`: every slab row is named by exactly one loader row. The loader rows on device d (in the order dp, ctx) name slab rows of window d // 128 only; each loader device's 288 rows name exactly 256 slab rows; to each block of 256 slab rows that starts at a multiple of 256, one loader device sends either exactly 4 rows or none.
All inputs are finite; a program needn't handle non-finite values.
Results may differ from the reference program's by a relative error of at most 0.025.
Values may be sent and summed in bfloat16 or wider, within the bound.
A program may use at most 64 MiB of HBM per device.

```python
import math
import jax
import jax.numpy as jnp
import numpy as np
from jax import lax

HEADS = 16
KV_HEADS = 4
HEAD_DIM = 128
TOK_DEV = 256
LOAD_DEV = 288
CAP = 4
WINDOW = 32768
MOST = 512
SPAN = 2
DOCS = 96
ROWS = 131072
LOADS = 147456
N_DP = 4
N_CTX = 128


def window_slab_rows(window_key, window_index):
    half = N_CTX // 2
    loader_rank = jax.random.permutation(jax.random.fold_in(window_key, 1), N_CTX).astype(jnp.int32)
    owner_rank = jax.random.permutation(jax.random.fold_in(window_key, 2), N_CTX).astype(jnp.int32)
    inverse = jnp.zeros((N_CTX,), jnp.int32).at[owner_rank].set(jnp.arange(N_CTX, dtype=jnp.int32))
    turn_index = jnp.arange(half, dtype=jnp.int32)
    owner_of = inverse[(turn_index[None, :] - loader_rank[:, None]) % N_CTX]
    key_limit = 2 ** 30 // TOK_DEV
    owner_scores = jax.random.randint(jax.random.fold_in(window_key, 3), (N_CTX, TOK_DEV), 0, key_limit) * TOK_DEV
    owner_scores = owner_scores + jnp.arange(TOK_DEV, dtype=jnp.int32)[None, :]
    owner_order = jnp.argsort(owner_scores, axis=1).astype(jnp.int32)
    entry_index = turn_index[:, None] * CAP + jnp.arange(CAP, dtype=jnp.int32)[None, :]
    local_row = owner_order[owner_of[:, :, None], entry_index[None, :, :]]
    target = (window_index * WINDOW + owner_of[:, :, None] * TOK_DEV + local_row).reshape(N_CTX, TOK_DEV)
    row_limit = 2 ** 30 // LOAD_DEV
    row_scores = jax.random.randint(jax.random.fold_in(window_key, 4), (N_CTX, LOAD_DEV), 0, row_limit) * LOAD_DEV
    row_scores = row_scores + jnp.arange(LOAD_DEV, dtype=jnp.int32)[None, :]
    row_order = jnp.argsort(row_scores, axis=1).astype(jnp.int32)[:, :TOK_DEV]
    result = jnp.full((N_CTX, LOAD_DEV), -1, jnp.int32)
    result = result.at[jnp.arange(N_CTX, dtype=jnp.int32)[:, None], row_order].set(target)
    return result


def draw_slab_row(key, part):
    windows = jnp.arange(N_DP, dtype=jnp.int32)
    window_keys = jax.vmap(lambda index: jax.random.fold_in(key, 100 + index))(windows)
    result = jax.vmap(window_slab_rows)(window_keys, windows)
    return result.reshape(N_DP * N_CTX * LOAD_DEV)


def draw_queries(key, part):
    shape_rows = (LOADS, HEADS * HEAD_DIM)
    return jnp.clip(jax.random.normal(jax.random.fold_in(key, 24), shape_rows, jnp.float32), -6.0, 6.0).astype(jnp.bfloat16)


def draw_key_rows(key, part):
    shape_rows = (LOADS, KV_HEADS * HEAD_DIM)
    return jnp.clip(jax.random.normal(jax.random.fold_in(key, 34), shape_rows, jnp.float32), -6.0, 6.0).astype(jnp.bfloat16)


def block_scale(key, shape, split, least, top_value):
    def one(position, shards_of):
        heights = jax.random.uniform(jax.random.fold_in(jax.random.fold_in(key, 6), position), (shards_of,), jnp.float32, least / len(split), top_value / len(split))
        return jnp.repeat(jnp.exp(heights), shape[position] // shards_of).reshape((-1,) + (1,) * (len(shape) - position - 1))

    loudness = one(*split[0])
    for cut in split[1:]:
        loudness = loudness * one(*cut)
    return loudness


def split_up(number_of, total, limit, slope):
    portions = [(1 << 20) // math.isqrt(standing ** slope) + 1 for standing in range(2, number_of + 1)]
    surplus, counts = total - limit - (number_of - 1), [1] * (number_of - 1)
    while surplus > 0:
        candidates = [i for i in range(number_of - 1) if counts[i] < limit]
        pool, remaining = sum([portions[i] for i in candidates]), surplus
        for i in candidates:
            addition = min(limit - counts[i], max(1, remaining * portions[i] // pool), surplus)
            counts[i] = counts[i] + addition
            surplus = surplus - addition
    return np.array([limit] + counts)


def ragged(own_key, amount, total, bound, lean):
    if amount == 2:
        one = jax.random.randint(own_key, (), max(1, total - bound), min(bound, total - 1) + 1)
        return jnp.stack([one, total - one])
    sizes = jnp.asarray(split_up(amount, total, bound, lean), jnp.int32)
    couples = (amount - 1) // 2
    donor, receiver = sizes[1:1 + 2 * couples:2], sizes[2:2 + 2 * couples:2]
    slack = jnp.minimum(donor - 1, bound - receiver)
    moved = jax.random.randint(jax.random.fold_in(own_key, 1), (couples,), 0, 1 << 20) % (slack + 1)
    sizes = sizes.at[1:1 + 2 * couples:2].set(donor - moved).at[2:2 + 2 * couples:2].set(receiver + moved)
    return sizes[jax.random.permutation(jax.random.fold_in(own_key, 2), amount)]


def noise(stream_key, shape, spread, most, shards=(), held_as=jnp.bfloat16):
    entries = jax.random.normal(stream_key, shape, jnp.float32) * spread
    if len(shards) > 0:
        entries = block_scale(stream_key, shape, shards, -0.22, 0.18) * entries
    return jnp.clip(entries, min=-most, max=most).astype(held_as)


def setup_inputs(seed: int = 0) -> dict:
    arg_keys = jax.random.split(jax.random.key(seed), 7)
    queries = draw_queries(jax.random.fold_in(arg_keys[6], 71), 0)
    key_rows = draw_key_rows(jax.random.fold_in(arg_keys[6], 71), 0)
    value_rows = noise(arg_keys[2], (LOADS, KV_HEADS * HEAD_DIM), 1.0, 6.0, ((0, 512),))
    slab_row = draw_slab_row(jax.random.fold_in(arg_keys[6], 71), 0)
    doc_lengths = jax.vmap(lambda own: ragged(own, DOCS, WINDOW, MOST, 2))(jax.random.split(arg_keys[4], N_DP)).reshape((N_DP, DOCS)).astype(jnp.int32)
    out_grad = noise(arg_keys[5], (ROWS, HEADS * HEAD_DIM), 1.0, 6.0, ((0, 512),))
    return {"queries": queries, "key_rows": key_rows, "value_rows": value_rows, "slab_row": slab_row, "doc_lengths": doc_lengths, "out_grad": out_grad}


MASKED = -1.0e30


def lowered(values_in):
    return lax.optimization_barrier(values_in.astype(jnp.bfloat16)).astype(jnp.float32)


def window_grads(query_win, key_win, value_win, grad_win, lengths):
    reach = SPAN * TOK_DEV
    key_count = reach + TOK_DEV
    doc_ends = jnp.cumsum(lengths)
    key_pad = jnp.concatenate([jnp.zeros((reach, KV_HEADS, HEAD_DIM), key_win.dtype), key_win], axis=0)
    value_pad = jnp.concatenate([jnp.zeros((reach, KV_HEADS, HEAD_DIM), value_win.dtype), value_win], axis=0)
    score_scale = HEAD_DIM ** -0.5

    def block_step(totals, block_index):
        key_acc, value_acc = totals
        offset = block_index * TOK_DEV
        query_blk = lax.dynamic_slice_in_dim(query_win, offset, TOK_DEV, 0).astype(jnp.float32)
        grad_blk = lax.dynamic_slice_in_dim(grad_win, offset, TOK_DEV, 0).astype(jnp.float32)
        key_blk = lax.dynamic_slice_in_dim(key_pad, offset, key_count, 0).astype(jnp.float32)
        value_blk = lax.dynamic_slice_in_dim(value_pad, offset, key_count, 0).astype(jnp.float32)
        query_pos = offset + jnp.arange(TOK_DEV, dtype=jnp.int32)
        key_pos = offset - reach + jnp.arange(key_count, dtype=jnp.int32)
        doc_start = jnp.sum(jnp.where(doc_ends[None, :] <= query_pos[:, None], lengths[None, :], 0), axis=1)
        allowed = (key_pos[None, :] >= doc_start[:, None]) & (key_pos[None, :] <= query_pos[:, None])
        score = jnp.einsum("qhgd,khd->hgqk", query_blk, key_blk) * score_scale
        score = jnp.where(allowed, score, MASKED)
        row_max = jnp.max(score, axis=3, keepdims=True)
        row_sum = jnp.sum(jnp.exp(score - row_max), axis=3, keepdims=True)
        log_norm = row_max + jnp.log(row_sum)
        weights = jnp.where(allowed, jnp.exp(score - log_norm), 0.0)
        weights_low = lowered(weights)
        attended = lowered(jnp.einsum("hgqk,khd->qhgd", weights_low, value_blk))
        row_dot = jnp.sum(grad_blk * attended, axis=3)
        grad_weights = jnp.einsum("qhgd,khd->hgqk", grad_blk, value_blk)
        grad_score = lowered(weights * (grad_weights - jnp.transpose(row_dot, (1, 2, 0))[..., None]))
        grad_query = jnp.einsum("hgqk,khd->qhgd", grad_score, key_blk) * score_scale
        key_part = lowered(jnp.einsum("hgqk,qhgd->khd", grad_score, query_blk) * score_scale)
        value_part = lowered(jnp.einsum("hgqk,qhgd->khd", weights_low, grad_blk))
        key_acc = lax.dynamic_update_slice_in_dim(
            key_acc, lax.dynamic_slice_in_dim(key_acc, offset, key_count, 0) + key_part, offset, 0)
        value_acc = lax.dynamic_update_slice_in_dim(
            value_acc, lax.dynamic_slice_in_dim(value_acc, offset, key_count, 0) + value_part, offset, 0)
        return (key_acc, value_acc), grad_query.astype(jnp.bfloat16)

    initial = jnp.zeros((reach + WINDOW, KV_HEADS, HEAD_DIM), jnp.float32)
    (key_acc, value_acc), grad_blocks = lax.scan(block_step, (initial, initial), jnp.arange(N_CTX, dtype=jnp.int32))
    grad_query = grad_blocks.reshape(WINDOW, HEADS * HEAD_DIM)
    grad_key = key_acc[reach:].astype(jnp.bfloat16).reshape(WINDOW, KV_HEADS * HEAD_DIM)
    grad_value = value_acc[reach:].astype(jnp.bfloat16).reshape(WINDOW, KV_HEADS * HEAD_DIM)
    return grad_query, grad_key, grad_value


def reference(queries, key_rows, value_rows, slab_row, doc_lengths, out_grad):
    total_rows = N_DP * WINDOW
    groups = HEADS // KV_HEADS
    target = jnp.where(slab_row >= 0, slab_row, total_rows).astype(jnp.int32)

    def place(row_data):
        buffer = jnp.zeros((total_rows, row_data.shape[1]), row_data.dtype)
        return buffer.at[target].set(row_data, mode="drop")

    query_all = place(queries).reshape(N_DP, WINDOW, KV_HEADS, groups, HEAD_DIM)
    key_all = place(key_rows).reshape(N_DP, WINDOW, KV_HEADS, HEAD_DIM)
    value_all = place(value_rows).reshape(N_DP, WINDOW, KV_HEADS, HEAD_DIM)
    grad_all = out_grad.reshape(N_DP, WINDOW, KV_HEADS, groups, HEAD_DIM)
    query_out = []
    key_out = []
    value_out = []
    for window_index in range(N_DP):
        grad_query, grad_key, grad_value = window_grads(
            query_all[window_index], key_all[window_index], value_all[window_index],
            grad_all[window_index], doc_lengths[window_index])
        query_out.append(grad_query)
        key_out.append(grad_key)
        value_out.append(grad_value)
    return (jnp.concatenate(query_out, axis=0), jnp.concatenate(key_out, axis=0), jnp.concatenate(value_out, axis=0))
```

```python
import functools

import jax
import jax.numpy as jnp
from jax import lax
from jax.experimental import pallas as pl
from jax.experimental.pallas import tpu as pltpu
from jax.sharding import PartitionSpec as P

HEADS = 16
KV_HEADS = 4
HEAD_DIM = 128
TOK = 256
LOAD = 288
LOAD_PAD = 384
PLANE = 8
NZ = 16
SLAB = PLANE * TOK
HALO = 512
MASKED = -1e30
SCALE = HEAD_DIM ** (-0.5)
MESH = pl.DeviceIdType.MESH
BF16 = jnp.bfloat16
F32 = jnp.float32


def dot(a, b, contract=((1,), (0,))):
    return lax.dot_general(a, b, (contract, ((), ())), preferred_element_type=F32)


def kernel(q_ref, k_ref, v_ref, slot_ref, pos_ref, grad_ref, low_ref, dq_ref, dkv_ref,
           xa0, xa12, slots, gslab, onehot, zs, rs, zr, rr, place, kv, acc, dqs, hs, hr, ps, pr,
           outs, sem_as, sem_ar, sem_zs, sem_zr, sem_es, sem_er):
    dp = lax.axis_index("dp")
    me = lax.axis_index("ctx")
    z = me // PLANE
    j = me % PLANE
    x = j // 2
    c = j % 2
    other = j + 1 - 2 * c
    up = (z + 1) % NZ
    down = (z + NZ - 1) % NZ

    xa0[:, LOAD:, :] = jnp.zeros((PLANE, LOAD_PAD - LOAD, 256), BF16)
    xa12[:, LOAD:, :] = jnp.zeros((PLANE, LOAD_PAD - LOAD, 256), BF16)

    barrier = pltpu.get_barrier_semaphore()
    peers = [(z, (j + d) % PLANE) for d in range(1, PLANE)]
    peers += [((z + d) % NZ, j) for d in range(1, NZ)]
    peers += [(up, other), (down, other)]
    for pz, pj in peers:
        pl.semaphore_signal(barrier, inc=1, device_id=(dp, pz * PLANE + pj), device_id_type=MESH)
    pl.semaphore_wait(barrier, len(peers))

    def remote(src, dst, send, recv, pz, pj):
        pltpu.make_async_remote_copy(
            src_ref=src, dst_ref=dst, send_sem=send, recv_sem=recv,
            device_id=(dp, pz * PLANE + pj), device_id_type=MESH).start()

    def local(src, dst, sem):
        pltpu.make_async_copy(src, dst, sem).start()

    def await_bytes(ref, sem):
        pltpu.make_async_copy(ref, ref, sem).wait()

    rows = pl.ds(0, LOAD)

    def kv_dst():
        return xa0.at[j, rows, pl.ds(0, 128)]

    def pos_dst():
        return xa0.at[j, rows, pl.ds(128, 128)]

    def slot_dst():
        return slots.at[j]

    def q_dst():
        return xa12.at[j, rows, :]

    def grad_dst():
        return gslab.at[pl.ds(pl.multiple_of(j * TOK, TOK), TOK), :]

    def kv_column(pj):
        return pl.ds(pl.multiple_of((pj // 2) * 128, 128), 128)

    def wide_column(pj):
        return pl.ds(pl.multiple_of(pj * 256, 128), 256)

    for d in range(1, PLANE):
        pj = (j + d) % PLANE
        remote(slot_ref, slot_dst(), sem_as.at[0], sem_ar.at[0], z, pj)

        @pl.when(pj % 2 == 0)
        def _():
            remote(k_ref.at[:, kv_column(pj)], kv_dst(), sem_as.at[1], sem_ar.at[1], z, pj)

        @pl.when(pj % 2 == 1)
        def _():
            remote(v_ref.at[:, kv_column(pj)], kv_dst(), sem_as.at[1], sem_ar.at[1], z, pj)

        remote(pos_ref, pos_dst(), sem_as.at[2], sem_ar.at[2], z, pj)
    local(slot_ref, slot_dst(), sem_ar.at[0])

    @pl.when(c == 0)
    def _():
        local(k_ref.at[:, kv_column(j)], kv_dst(), sem_ar.at[1])

    @pl.when(c == 1)
    def _():
        local(v_ref.at[:, kv_column(j)], kv_dst(), sem_ar.at[1])

    local(pos_ref, pos_dst(), sem_ar.at[2])
    for d in range(1, PLANE):
        pj = (j + d) % PLANE
        remote(q_ref.at[:, wide_column(pj)], q_dst(), sem_as.at[3], sem_ar.at[3], z, pj)
    local(q_ref.at[:, wide_column(j)], q_dst(), sem_ar.at[3])
    for d in range(1, PLANE):
        pj = (j + d) % PLANE
        remote(grad_ref.at[:, wide_column(pj)], grad_dst(), sem_as.at[4], sem_ar.at[4], z, pj)
    local(grad_ref.at[:, wide_column(j)], grad_dst(), sem_ar.at[4])

    acc[...] = jnp.zeros_like(acc)

    def plane_of(d):
        return (z + ((d + 1) // 2) * (2 * (d % 2) - 1) + NZ) % NZ

    await_bytes(slots, sem_ar.at[0])
    await_bytes(xa0.at[:, rows, pl.ds(0, 128)], sem_ar.at[1])
    await_bytes(xa0.at[:, rows, pl.ds(128, 128)], sem_ar.at[2])

    def pack_first(zp):
        row = lax.broadcasted_iota(jnp.int32, (128, 4 * LOAD_PAD), 0) + zp * 128
        for quad in range(2):
            wanted = jnp.concatenate([slots[quad * 4 + i, 0:1, :] for i in range(4)], axis=1)
            hot = jnp.where(row == wanted, 1.0, 0.0).astype(BF16)
            onehot[zp, quad] = hot
            block = xa0[quad * 4:quad * 4 + 4].reshape(4 * LOAD_PAD, 256)
            packed = dot(hot, block)
            zs[0, zp, :, quad] = packed[:, :128].astype(BF16).reshape(PLANE, 16, 128)
            rs[zp, quad] = jnp.sum(packed[:, 128:].reshape(PLANE, 16, 128), axis=0).astype(BF16)

    @pl.loop(1, NZ)
    def _(d):
        zp = plane_of(d)
        pack_first(zp)
        remote(zs.at[0, zp], zr.at[0, :, :, z], sem_zs.at[0], sem_zr.at[0], zp, j)
        remote(rs.at[zp], rr.at[:, z], sem_zs.at[1], sem_zr.at[1], zp, j)

    pack_first(z)
    local(zs.at[0, z], zr.at[0, :, :, z], sem_zr.at[0])
    local(rs.at[z], rr.at[:, z], sem_zr.at[1])

    await_bytes(xa12.at[:, rows, :], sem_ar.at[3])

    def pack_second(zp):
        for quad in range(2):
            block = xa12[quad * 4:quad * 4 + 4].reshape(4 * LOAD_PAD, 256)
            packed = dot(onehot[zp, quad], block).astype(BF16)
            zs[1, zp, :, quad] = packed[:, :128].reshape(PLANE, 16, 128)
            zs[2, zp, :, quad] = packed[:, 128:].reshape(PLANE, 16, 128)

    @pl.loop(1, NZ)
    def _(d):
        zp = plane_of(d)
        pack_second(zp)
        remote(zs.at[1, zp], zr.at[1, :, :, z], sem_zs.at[2], sem_zr.at[2], zp, j)

    pack_second(z)
    local(zs.at[1, z], zr.at[1, :, :, z], sem_zr.at[2])

    await_bytes(rr, sem_zr.at[1])
    marks = [jnp.transpose(rr[quad].reshape(NZ * 16, 128).astype(F32)) for quad in range(2)]
    spot = lax.broadcasted_iota(jnp.int32, (TOK, 2 * NZ * 16), 0).astype(F32) + 1.0
    for o in range(PLANE):
        mark = jnp.concatenate([marks[0][o:o + 1], marks[1][o:o + 1]], axis=1)
        place[o] = jnp.where(spot == mark, 1.0, 0.0).astype(BF16)

    def settle(chunk, o):
        return dot(place[o], zr[chunk, o].reshape(2 * NZ * 16, 128)).astype(BF16)

    await_bytes(zr.at[0], sem_zr.at[0])

    @pl.loop(0, PLANE)
    def _(o):
        kv[c, pl.ds(pl.multiple_of(HALO + o * TOK, TOK), TOK), :] = settle(0, o)

    own_kv = kv.at[c, pl.ds(HALO, SLAB), :]
    remote(own_kv, own_kv, sem_es.at[0], sem_er.at[0], z, other)
    tail = kv.at[c, pl.ds(SLAB, HALO), :]
    head = kv.at[c, pl.ds(0, HALO), :]
    remote(tail, head, sem_es.at[1], sem_er.at[1], up, j)
    remote(tail, head, sem_es.at[1], sem_er.at[1], up, other)

    for part in range(4):
        pair = pl.ds(2 * part, 2)

        @pl.loop(1, NZ)
        def _(d):
            zp = plane_of(d)
            remote(zs.at[2, zp, pair], zr.at[2, pair, :, z], sem_zs.at[3], sem_zr.at[3 + part], zp, j)

        local(zs.at[2, z, pair], zr.at[2, pair, :, z], sem_zr.at[3 + part])

    await_bytes(own_kv, sem_er.at[0])
    await_bytes(kv.at[:, pl.ds(0, HALO), :], sem_er.at[1])
    await_bytes(gslab, sem_ar.at[4])

    def attend(head_index, b):
        window = pl.ds(pl.multiple_of(b * TOK, TOK), HALO + TOK)
        query = settle(1 + head_index, b)
        grad = gslab[pl.ds(pl.multiple_of(b * TOK, TOK), TOK), head_index * 128:head_index * 128 + 128]
        keys = kv[0, window, :]
        values = kv[1, window, :]
        key_index = lax.broadcasted_iota(jnp.int32, (HALO + TOK, TOK), 0)
        query_index = lax.broadcasted_iota(jnp.int32, (HALO + TOK, TOK), 1)
        allowed = (key_index >= low_ref[b]) & (key_index <= query_index + HALO)
        score = dot(keys, query, ((1,), (1,)))
        score = jnp.where(allowed, score, MASKED)
        top = jnp.max(score, axis=0, keepdims=True)
        weights = jnp.exp((score - top) * SCALE)
        weights = weights * (1.0 / jnp.sum(weights, axis=0, keepdims=True))
        grad_weights = dot(values, grad, ((1,), (1,)))
        row_dot = jnp.sum(weights * grad_weights, axis=0, keepdims=True)
        grad_score = (weights * (grad_weights - row_dot)).astype(BF16)
        acc[1, window, :] += dot(weights.astype(BF16), grad)
        acc[0, window, :] += dot(grad_score, query) * SCALE
        dqs[head_index, b] = (dot(grad_score, keys, ((0,), (0,))) * SCALE).astype(BF16)
        column = pl.ds(pl.multiple_of(j * 256 + head_index * 128, 128), 128)

        @pl.when(b == j)
        def _():
            local(dqs.at[head_index, b], dq_ref.at[:, column], sem_er.at[2])

        @pl.when(b != j)
        def _():
            remote(dqs.at[head_index, b], dq_ref.at[:, column], sem_es.at[2], sem_er.at[2], z, b)

    await_bytes(zr.at[1], sem_zr.at[2])

    @pl.loop(0, PLANE)
    def _(b):
        attend(0, b)

    for part in range(4):
        await_bytes(zr.at[2, pl.ds(2 * part, 2)], sem_zr.at[3 + part])

        @pl.loop(2 * part, 2 * part + 2)
        def _(b):
            attend(1, b)

        if part == 0:
            hs[...] = acc[:, :HALO, :].astype(BF16)
            remote(hs, hr, sem_es.at[3], sem_er.at[3], down, j)

    await_bytes(hr, sem_er.at[3])
    acc[:, SLAB:, :] += hr[...].astype(F32)
    ps[...] = acc[1 - c, HALO:, :].astype(BF16)
    remote(ps, pr, sem_es.at[4], sem_er.at[4], z, other)
    await_bytes(pr, sem_er.at[4])
    outs[...] = (acc[c, HALO:, :] + pr[...].astype(F32)).astype(BF16).reshape(PLANE, TOK, 128)
    column = pl.ds(pl.multiple_of(x * 128, 128), 128)
    for d in range(1, PLANE):
        pj = (j + d) % PLANE
        remote(outs.at[pj], dkv_ref.at[c, :, column], sem_es.at[5], sem_er.at[5], z, pj)
    local(outs.at[j], dkv_ref.at[c, :, column], sem_er.at[5])

    seven = pl.ds(0, PLANE - 1)
    await_bytes(dkv_ref, sem_er.at[5])
    await_bytes(dq_ref, sem_er.at[2])
    await_bytes(slots.at[seven], sem_as.at[0])
    await_bytes(xa0.at[seven, rows, pl.ds(0, 128)], sem_as.at[1])
    await_bytes(xa0.at[seven, rows, pl.ds(128, 128)], sem_as.at[2])
    await_bytes(xa12.at[seven, rows, :], sem_as.at[3])
    await_bytes(gslab.at[pl.ds(0, 7 * TOK), :], sem_as.at[4])
    most = pl.ds(0, NZ - 1)
    await_bytes(zs.at[0, most], sem_zs.at[0])
    await_bytes(rs.at[most], sem_zs.at[1])
    await_bytes(zs.at[1, most], sem_zs.at[2])
    await_bytes(zs.at[2, most], sem_zs.at[3])
    await_bytes(own_kv, sem_es.at[0])
    await_bytes(kv.at[:, pl.ds(0, HALO), :], sem_es.at[1])
    await_bytes(dqs.at[:, seven], sem_es.at[2])
    await_bytes(hs, sem_es.at[3])
    await_bytes(ps, sem_es.at[4])
    await_bytes(outs.at[seven], sem_es.at[5])


def body(queries, key_rows, value_rows, slab_row, doc_lengths, out_grad):
    me = lax.axis_index("ctx")
    z = me // PLANE
    j = me % PLANE
    kept = slab_row >= 0
    owner = jnp.where(kept, slab_row // TOK % (NZ * PLANE), -1)
    order = jnp.arange(LOAD, dtype=jnp.int32)
    earlier = (owner[:, None] == owner[None, :]) & (order[:, None] < order[None, :])
    rank = jnp.sum(earlier.astype(jnp.int32), axis=0)
    slot = jnp.where(kept, owner * 16 + (j % 4) * 4 + rank, -1)
    slot = jnp.pad(slot, (0, LOAD_PAD - LOAD), constant_values=-1)
    slot = jnp.broadcast_to(slot[None, :], (8, LOAD_PAD))
    lane = jnp.arange(128, dtype=jnp.int32)
    mark = jnp.where(kept, slab_row % TOK + 1, 0)
    pos = jnp.where(lane[None, :] == (owner % PLANE)[:, None], mark[:, None], 0).astype(BF16)
    lengths = doc_lengths[0]
    doc_ends = jnp.cumsum(lengths)
    position = z * SLAB + jnp.arange(SLAB, dtype=jnp.int32)
    doc_start = jnp.sum(
        jnp.where(doc_ends[:, None] <= position[None, :], lengths[:, None], 0), axis=0
    ).reshape(PLANE, 1, TOK)
    base = z * SLAB + jnp.arange(PLANE, dtype=jnp.int32) * TOK - HALO
    low = doc_start - base[:, None, None]
    any_spec = pl.BlockSpec(memory_space=pl.ANY)
    vmem_spec = pl.BlockSpec(memory_space=pltpu.VMEM)
    dq, dkv = pl.pallas_call(
        kernel,
        out_shape=(
            jax.ShapeDtypeStruct((TOK, HEADS * HEAD_DIM), BF16),
            jax.ShapeDtypeStruct((2, TOK, KV_HEADS * HEAD_DIM), BF16),
        ),
        in_specs=[any_spec] * 6 + [vmem_spec],
        out_specs=(any_spec, any_spec),
        scratch_shapes=[
            pltpu.VMEM((PLANE, LOAD_PAD, 256), BF16),
            pltpu.VMEM((PLANE, LOAD_PAD, 256), BF16),
            pltpu.VMEM((PLANE, 8, LOAD_PAD), jnp.int32),
            pltpu.VMEM((SLAB, 256), BF16),
            pltpu.VMEM((NZ, 2, 128, 4 * LOAD_PAD), BF16),
            pltpu.VMEM((3, NZ, PLANE, 2, 16, 128), BF16),
            pltpu.VMEM((NZ, 2, 16, 128), BF16),
            pltpu.VMEM((3, PLANE, 2, NZ, 16, 128), BF16),
            pltpu.VMEM((2, NZ, 16, 128), BF16),
            pltpu.VMEM((PLANE, TOK, 2 * NZ * 16), BF16),
            pltpu.VMEM((2, HALO + SLAB, 128), BF16),
            pltpu.VMEM((2, HALO + SLAB, 128), F32),
            pltpu.VMEM((2, PLANE, TOK, 128), BF16),
            pltpu.VMEM((2, HALO, 128), BF16),
            pltpu.VMEM((2, HALO, 128), BF16),
            pltpu.VMEM((SLAB, 128), BF16),
            pltpu.VMEM((SLAB, 128), BF16),
            pltpu.VMEM((PLANE, TOK, 128), BF16),
            pltpu.SemaphoreType.DMA((5,)),
            pltpu.SemaphoreType.DMA((5,)),
            pltpu.SemaphoreType.DMA((4,)),
            pltpu.SemaphoreType.DMA((7,)),
            pltpu.SemaphoreType.DMA((6,)),
            pltpu.SemaphoreType.DMA((6,)),
        ],
        compiler_params=pltpu.CompilerParams(
            collective_id=0, has_side_effects=True, vmem_limit_bytes=60 * 1024 * 1024
        ),
        name="packed_attention",
    )(queries, key_rows, value_rows, slot, pos, out_grad, low)
    return (dq, dkv[0], dkv[1])


def solution(mesh):
    in_specs = (
        P(("dp", "ctx"), None),
        P(("dp", "ctx"), None),
        P(("dp", "ctx"), None),
        P(("dp", "ctx")),
        P("dp", None),
        P(("dp", "ctx"), None),
    )
    out_specs = (P(("dp", "ctx"), None), P(("dp", "ctx"), None), P(("dp", "ctx"), None))
    return jax.shard_map(body, mesh=mesh, in_specs=in_specs, out_specs=out_specs, check_vma=False)
```

```python
import functools

import jax
import jax.numpy as jnp
from jax import lax
from jax.experimental import pallas as pl
from jax.experimental.pallas import tpu as pltpu
from jax.sharding import PartitionSpec as P

HEADS = 16
KV_HEADS = 4
HEAD_DIM = 128
TOK = 256
LOAD = 288
LOAD_PAD = 384
PLANE = 8
NZ = 16
SLAB = PLANE * TOK
HALO = 512
DOCS = 96
MASKED = -1e30
SCALE = HEAD_DIM ** (-0.5)
MESH = pl.DeviceIdType.MESH
BF16 = jnp.bfloat16
F32 = jnp.float32


def dot(a, b, contract=((1,), (0,))):
    return lax.dot_general(a, b, (contract, ((), ())), preferred_element_type=F32)


def kernel(q_ref, k_ref, v_ref, grad_ref, slab_ref, len_ref, dq_ref, dk_ref, dv_ref,
           slot_out, pos_out, low, xk, xq, slots, gslab, onehot, zs, rs, zr, rr, place, kv, acc,
           dqs, hs, hr, ps, pr, outs, sem_as, sem_ar, sem_zs, sem_zr, sem_es, sem_er, sem_pr):
    dp = lax.axis_index("dp")
    me = lax.axis_index("ctx")
    z = me // PLANE
    j = me % PLANE
    x = j // 2
    c = j % 2
    other = j + 1 - 2 * c
    up = (z + 1) % NZ
    down = (z + NZ - 1) % NZ

    barrier = pltpu.get_barrier_semaphore()
    peers = [(z, (j + d) % PLANE) for d in range(1, PLANE)]
    peers += [((z + d) % NZ, j) for d in range(1, NZ)]
    peers += [(up, other), (down, other)]
    for pz, pj in peers:
        pl.semaphore_signal(barrier, inc=1, device_id=(dp, pz * PLANE + pj), device_id_type=MESH)

    xk[:, LOAD:, :] = jnp.zeros((PLANE, LOAD_PAD - LOAD, 128), BF16)
    xq[:, LOAD:, :] = jnp.zeros((PLANE, LOAD_PAD - LOAD, 384), BF16)
    slab = slab_ref[0:1, :]
    kept = slab >= 0
    owner = jnp.where(kept, (slab >> 8) & (NZ * PLANE - 1), -1)
    owner_f = owner.astype(F32)
    seat_f = jnp.where(kept, owner & (PLANE - 1), -1).astype(F32)
    mark_f = jnp.where(kept, (slab & (TOK - 1)) + 1, 0).astype(F32)
    lane = lax.broadcasted_iota(jnp.int32, (128, LOAD_PAD), 1)
    line = lax.broadcasted_iota(jnp.int32, (128, LOAD_PAD), 0)
    rank = jnp.zeros((1, LOAD_PAD), F32)
    seat_lane = lax.broadcasted_iota(jnp.int32, (128, 128), 1).astype(F32)
    for k in range(3):
        tile = slice(128 * k, 128 * k + 128)
        owner_col = jnp.transpose(jnp.broadcast_to(owner_f[:, tile], (LOAD_PAD, 128)))
        before = (owner_col == owner_f) & (line + 128 * k < lane)
        rank = rank + jnp.sum(jnp.where(before, 1.0, 0.0), axis=0, keepdims=True)
        seat_col = jnp.transpose(jnp.broadcast_to(seat_f[:, tile], (128, 128)))
        mark_col = jnp.transpose(jnp.broadcast_to(mark_f[:, tile], (128, 128)))
        count = min(128, LOAD - 128 * k)
        pos = jnp.where(seat_lane == seat_col, mark_col, 0.0).astype(BF16)
        pos_out[128 * k:128 * k + count, :] = pos[:count]
    slot = jnp.where(kept, owner * 16 + (j % 4) * 4 + rank.astype(jnp.int32), -1)
    slot_out[...] = jnp.broadcast_to(slot, (8, LOAD_PAD))

    pl.semaphore_wait(barrier, len(peers))

    def remote(src, dst, send, recv, pz, pj):
        pltpu.make_async_remote_copy(
            src_ref=src, dst_ref=dst, send_sem=send, recv_sem=recv,
            device_id=(dp, pz * PLANE + pj), device_id_type=MESH).start()

    def local(src, dst, sem):
        pltpu.make_async_copy(src, dst, sem).start()

    def await_bytes(ref, sem):
        pltpu.make_async_copy(ref, ref, sem).wait()

    rows = pl.ds(0, LOAD)
    q_lanes = pl.ds(0, 256)
    pos_lanes = pl.ds(256, 128)

    def kv_dst():
        return xk.at[j, rows, :]

    def pos_dst():
        return xq.at[j, rows, pos_lanes]

    def q_dst():
        return xq.at[j, rows, q_lanes]

    def grad_dst():
        return gslab.at[pl.ds(pl.multiple_of(j * TOK, TOK), TOK), :]

    def kv_column(pj):
        return pl.ds(pl.multiple_of((pj // 2) * 128, 128), 128)

    def wide_column(pj):
        return pl.ds(pl.multiple_of(pj * 256, 128), 256)

    for d in range(1, PLANE):
        pj = (j + d) % PLANE

        @pl.when(pj % 2 == 0)
        def _():
            remote(k_ref.at[:, kv_column(pj)], kv_dst(), sem_as.at[1], sem_ar.at[1], z, pj)

        @pl.when(pj % 2 == 1)
        def _():
            remote(v_ref.at[:, kv_column(pj)], kv_dst(), sem_as.at[1], sem_ar.at[1], z, pj)

        remote(slot_out, slots.at[j], sem_as.at[0], sem_ar.at[0], z, pj)

    local(slot_out, slots.at[j], sem_ar.at[0])

    @pl.when(c == 0)
    def _():
        local(k_ref.at[:, kv_column(j)], kv_dst(), sem_ar.at[1])

    @pl.when(c == 1)
    def _():
        local(v_ref.at[:, kv_column(j)], kv_dst(), sem_ar.at[1])

    for d in range(1, PLANE):
        pj = (j + d) % PLANE
        remote(pos_out, pos_dst(), sem_as.at[2], sem_ar.at[2], z, pj)
        remote(q_ref.at[:, wide_column(pj)], q_dst(), sem_as.at[3], sem_ar.at[3], z, pj)
    local(pos_out, pos_dst(), sem_ar.at[2])
    local(q_ref.at[:, wide_column(j)], q_dst(), sem_ar.at[3])
    for d in range(1, PLANE):
        pj = (j + d) % PLANE
        remote(grad_ref.at[:, wide_column(pj)], grad_dst(), sem_as.at[4], sem_ar.at[4], z, pj)
    local(grad_ref.at[:, wide_column(j)], grad_dst(), sem_ar.at[4])

    def plane_of(d):
        return (z + ((d + 1) // 2) * (2 * (d % 2) - 1) + NZ) % NZ

    await_bytes(slots, sem_ar.at[0])
    await_bytes(xk.at[:, rows, :], sem_ar.at[1])

    def pack_first(zp):
        row = lax.broadcasted_iota(jnp.int32, (128, 4 * LOAD_PAD), 0) + zp * 128
        for quad in range(2):
            wanted = jnp.concatenate([slots[quad * 4 + i, 0:1, :] for i in range(4)], axis=1)
            hot = jnp.where(row == wanted, 1.0, 0.0).astype(BF16)
            onehot[zp, quad] = hot
            block = xk[quad * 4:quad * 4 + 4].reshape(4 * LOAD_PAD, 128)
            zs[0, zp, :, quad] = dot(hot, block).astype(BF16).reshape(PLANE, 16, 128)

    @pl.loop(1, NZ)
    def _(d):
        zp = plane_of(d)
        pack_first(zp)
        remote(zs.at[0, zp], zr.at[0, :, :, z], sem_zs.at[0], sem_zr.at[0], zp, j)

    pack_first(z)
    local(zs.at[0, z], zr.at[0, :, :, z], sem_zr.at[0])

    lengths = jnp.broadcast_to(len_ref[...].astype(F32), (DOCS, DOCS))
    doc_row = lax.broadcasted_iota(jnp.int32, (DOCS, DOCS), 0)
    doc_col = lax.broadcasted_iota(jnp.int32, (DOCS, DOCS), 1)
    doc_ends = jnp.sum(jnp.where(doc_col <= doc_row, lengths, 0.0), axis=1, keepdims=True)
    doc_size = jnp.sum(jnp.where(doc_col == doc_row, lengths, 0.0), axis=1, keepdims=True)
    offset = lax.broadcasted_iota(jnp.int32, (1, TOK), 1)
    for b in range(PLANE):
        place_at = (offset + (z * SLAB + b * TOK)).astype(F32)
        start = jnp.sum(jnp.where(doc_ends <= place_at, doc_size, 0.0), axis=0, keepdims=True)
        low[b] = start.astype(jnp.int32) - (z * SLAB + b * TOK - HALO)
    acc[...] = jnp.zeros_like(acc)

    await_bytes(xq.at[:, rows, pos_lanes], sem_ar.at[2])
    await_bytes(xq.at[:, rows, q_lanes], sem_ar.at[3])

    @pl.loop(0, NZ)
    def _(d):
        zp = plane_of(d)
        for quad in range(2):
            block = xq[quad * 4:quad * 4 + 4].reshape(4 * LOAD_PAD, 384)
            packed = dot(onehot[zp, quad], block)
            zs[1, zp, :, quad] = packed[:, :128].astype(BF16).reshape(PLANE, 16, 128)
            zs[2, zp, :, quad] = packed[:, 128:256].astype(BF16).reshape(PLANE, 16, 128)
            rs[zp, quad] = jnp.sum(packed[:, 256:].reshape(PLANE, 16, 128), axis=0).astype(BF16)

    for d in range(1, NZ):
        zp = plane_of(d)
        remote(rs.at[zp], rr.at[:, z], sem_zs.at[1], sem_zr.at[1], zp, j)
    local(rs.at[z], rr.at[:, z], sem_zr.at[1])
    for d in range(1, NZ):
        zp = plane_of(d)
        remote(zs.at[1, zp], zr.at[1, :, :, z], sem_zs.at[2], sem_zr.at[2], zp, j)
    local(zs.at[1, z], zr.at[1, :, :, z], sem_zr.at[2])

    await_bytes(rr, sem_zr.at[1])
    marks = [jnp.transpose(rr[quad].reshape(NZ * 16, 128).astype(F32)) for quad in range(2)]
    spot = lax.broadcasted_iota(jnp.int32, (TOK, 2 * NZ * 16), 0).astype(F32) + 1.0
    for o in range(PLANE):
        mark = jnp.concatenate([marks[0][o:o + 1], marks[1][o:o + 1]], axis=1)
        place[o] = jnp.where(spot == mark, 1.0, 0.0).astype(BF16)

    def settle(chunk, o):
        return dot(place[o], zr[chunk, o].reshape(2 * NZ * 16, 128)).astype(BF16)

    await_bytes(zr.at[0], sem_zr.at[0])

    @pl.loop(0, PLANE)
    def _(o):
        kv[c, pl.ds(pl.multiple_of(HALO + o * TOK, TOK), TOK), :] = settle(0, o)

    own_kv = kv.at[c, pl.ds(HALO, SLAB), :]
    remote(own_kv, own_kv, sem_es.at[0], sem_er.at[0], z, other)
    tail = kv.at[c, pl.ds(SLAB, HALO), :]
    head = kv.at[c, pl.ds(0, HALO), :]
    remote(tail, head, sem_es.at[1], sem_er.at[1], up, j)
    remote(tail, head, sem_es.at[1], sem_er.at[1], up, other)

    @pl.loop(0, PLANE)
    def _(o):
        @pl.loop(1, NZ)
        def _(d):
            zp = plane_of(d)
            remote(zs.at[2, zp, o], zr.at[2, o, :, z], sem_zs.at[3], sem_zr.at[3 + o], zp, j)

        local(zs.at[2, z, o], zr.at[2, o, :, z], sem_zr.at[3 + o])

    await_bytes(own_kv, sem_er.at[0])
    await_bytes(kv.at[:, pl.ds(0, HALO), :], sem_er.at[1])
    await_bytes(gslab, sem_ar.at[4])

    def attend(head_index, b):
        start = b * TOK if isinstance(b, int) else pl.multiple_of(b * TOK, TOK)
        window = pl.ds(start, HALO + TOK)
        query = settle(1 + head_index, b)
        grad = gslab[pl.ds(start, TOK), head_index * 128:head_index * 128 + 128]
        keys = kv[0, window, :]
        values = kv[1, window, :]
        key_index = lax.broadcasted_iota(jnp.int32, (HALO + TOK, TOK), 0)
        query_index = lax.broadcasted_iota(jnp.int32, (HALO + TOK, TOK), 1)
        allowed = (key_index >= low[b]) & (key_index <= query_index + HALO)
        score = dot(keys, query, ((1,), (1,)))
        score = jnp.where(allowed, score, MASKED)
        top = jnp.max(score, axis=0, keepdims=True)
        weights = jnp.exp((score - top) * SCALE)
        weights = weights * (1.0 / jnp.sum(weights, axis=0, keepdims=True))
        grad_weights = dot(values, grad, ((1,), (1,)))
        row_dot = jnp.sum(weights * grad_weights, axis=0, keepdims=True)
        grad_score = (weights * (grad_weights - row_dot)).astype(BF16)
        acc[1, window, :] += dot(weights.astype(BF16), grad)
        acc[0, window, :] += dot(grad_score, query) * SCALE
        dqs[head_index, b] = (dot(grad_score, keys, ((0,), (0,))) * SCALE).astype(BF16)
        column = pl.ds(pl.multiple_of(j * 256 + head_index * 128, 128), 128)

        @pl.when(j == b)
        def _():
            local(dqs.at[head_index, b], dq_ref.at[:, column], sem_er.at[2])

        @pl.when(j != b)
        def _():
            remote(dqs.at[head_index, b], dq_ref.at[:, column], sem_es.at[2], sem_er.at[2], z, b)

    def hand_over(t):
        ps[t] = acc[1 - c, HALO + t * TOK:HALO + t * TOK + TOK, :].astype(BF16)
        remote(ps.at[t], pr.at[t], sem_es.at[4], sem_pr.at[t], z, other)

    def finish(t):
        await_bytes(pr.at[t], sem_pr.at[t])
        total = acc[c, HALO + t * TOK:HALO + t * TOK + TOK, :] + pr[t].astype(F32)
        outs[t] = total.astype(BF16)
        column = pl.ds(pl.multiple_of(x * 128, 128), 128)
        for which, ref in ((0, dk_ref), (1, dv_ref)):
            @pl.when((c == which) & (j == t))
            def _():
                local(outs.at[t], ref.at[:, column], sem_er.at[4 + which])

            @pl.when((c == which) & (j != t))
            def _():
                remote(outs.at[t], ref.at[:, column], sem_es.at[5], sem_er.at[4 + which], z, t)

    await_bytes(zr.at[1], sem_zr.at[2])

    @pl.loop(0, PLANE)
    def _(b):
        attend(0, b)

    for b in range(PLANE):
        if b == PLANE - 1:
            await_bytes(hr, sem_er.at[3])
            acc[:, SLAB:, :] += hr[...].astype(F32)
        await_bytes(zr.at[2, b], sem_zr.at[3 + b])
        attend(1, b)
        if b == 1:
            hs[...] = acc[:, :HALO, :].astype(BF16)
            remote(hs, hr, sem_es.at[3], sem_er.at[3], down, j)
        if b >= 2:
            hand_over(b - 2)
        if b >= 3:
            finish(b - 3)
    hand_over(6)
    hand_over(7)
    for t in (5, 6, 7):
        finish(t)

    seven = pl.ds(0, PLANE - 1)
    most = pl.ds(0, NZ - 1)
    await_bytes(slots.at[seven], sem_as.at[0])
    await_bytes(xk.at[seven, rows, :], sem_as.at[1])
    await_bytes(xq.at[seven, rows, pos_lanes], sem_as.at[2])
    await_bytes(xq.at[seven, rows, q_lanes], sem_as.at[3])
    await_bytes(gslab.at[pl.ds(0, 7 * TOK), :], sem_as.at[4])
    await_bytes(zs.at[0, most], sem_zs.at[0])
    await_bytes(rs.at[most], sem_zs.at[1])
    await_bytes(zs.at[1, most], sem_zs.at[2])
    await_bytes(zs.at[2, most], sem_zs.at[3])
    await_bytes(own_kv, sem_es.at[0])
    await_bytes(kv.at[:, pl.ds(0, HALO), :], sem_es.at[1])
    await_bytes(dqs.at[:, seven], sem_es.at[2])
    await_bytes(hs, sem_es.at[3])
    await_bytes(ps, sem_es.at[4])
    await_bytes(outs.at[seven], sem_es.at[5])
    await_bytes(dq_ref, sem_er.at[2])
    await_bytes(dk_ref, sem_er.at[4])
    await_bytes(dv_ref, sem_er.at[5])


def body(queries, key_rows, value_rows, slab_row, doc_lengths, out_grad):
    slab = jnp.pad(slab_row, (0, LOAD_PAD - LOAD), constant_values=-1)
    slab = jnp.broadcast_to(slab[None, :], (8, LOAD_PAD))
    any_spec = pl.BlockSpec(memory_space=pl.ANY)
    vmem_spec = pl.BlockSpec(memory_space=pltpu.VMEM)
    return pl.pallas_call(
        kernel,
        out_shape=(
            jax.ShapeDtypeStruct((TOK, HEADS * HEAD_DIM), BF16),
            jax.ShapeDtypeStruct((TOK, KV_HEADS * HEAD_DIM), BF16),
            jax.ShapeDtypeStruct((TOK, KV_HEADS * HEAD_DIM), BF16),
        ),
        in_specs=[any_spec] * 4 + [vmem_spec] * 2,
        out_specs=(any_spec, any_spec, any_spec),
        scratch_shapes=[
            pltpu.VMEM((8, LOAD_PAD), jnp.int32),
            pltpu.VMEM((LOAD, 128), BF16),
            pltpu.VMEM((PLANE, 1, TOK), jnp.int32),
            pltpu.VMEM((PLANE, LOAD_PAD, 128), BF16),
            pltpu.VMEM((PLANE, LOAD_PAD, 384), BF16),
            pltpu.VMEM((PLANE, 8, LOAD_PAD), jnp.int32),
            pltpu.VMEM((SLAB, 256), BF16),
            pltpu.VMEM((NZ, 2, 128, 4 * LOAD_PAD), BF16),
            pltpu.VMEM((3, NZ, PLANE, 2, 16, 128), BF16),
            pltpu.VMEM((NZ, 2, 16, 128), BF16),
            pltpu.VMEM((3, PLANE, 2, NZ, 16, 128), BF16),
            pltpu.VMEM((2, NZ, 16, 128), BF16),
            pltpu.VMEM((PLANE, TOK, 2 * NZ * 16), BF16),
            pltpu.VMEM((2, HALO + SLAB, 128), BF16),
            pltpu.VMEM((2, HALO + SLAB, 128), F32),
            pltpu.VMEM((2, PLANE, TOK, 128), BF16),
            pltpu.VMEM((2, HALO, 128), BF16),
            pltpu.VMEM((2, HALO, 128), BF16),
            pltpu.VMEM((PLANE, TOK, 128), BF16),
            pltpu.VMEM((PLANE, TOK, 128), BF16),
            pltpu.VMEM((PLANE, TOK, 128), BF16),
            pltpu.SemaphoreType.DMA((5,)),
            pltpu.SemaphoreType.DMA((5,)),
            pltpu.SemaphoreType.DMA((4,)),
            pltpu.SemaphoreType.DMA((11,)),
            pltpu.SemaphoreType.DMA((6,)),
            pltpu.SemaphoreType.DMA((6,)),
            pltpu.SemaphoreType.DMA((8,)),
        ],
        compiler_params=pltpu.CompilerParams(
            collective_id=0, has_side_effects=True, vmem_limit_bytes=60 * 1024 * 1024
        ),
        name="packed_attention",
    )(queries, key_rows, value_rows, out_grad, slab, doc_lengths)


def solution(mesh):
    in_specs = (
        P(("dp", "ctx"), None),
        P(("dp", "ctx"), None),
        P(("dp", "ctx"), None),
        P(("dp", "ctx")),
        P("dp", None),
        P(("dp", "ctx"), None),
    )
    out_specs = (P(("dp", "ctx"), None), P(("dp", "ctx"), None), P(("dp", "ctx"), None))
    return jax.shard_map(body, mesh=mesh, in_specs=in_specs, out_specs=out_specs, check_vma=False)
```

```python
import functools

import jax
import jax.numpy as jnp
from jax import lax
from jax.experimental import pallas as pl
from jax.experimental.pallas import tpu as pltpu
from jax.sharding import PartitionSpec as P

HEADS = 16
KV_HEADS = 4
HEAD_DIM = 128
TOK = 256
LOAD = 288
LOAD_PAD = 384
PLANE = 8
NZ = 16
SLAB = PLANE * TOK
HALO = 512
DOCS = 96
NDP = 4
CAP = 176
MASKED = -1e30
SCALE = HEAD_DIM ** (-0.5)
MESH = pl.DeviceIdType.MESH
BF16 = jnp.bfloat16
F32 = jnp.float32


def dot(a, b, contract=((1,), (0,))):
    return lax.dot_general(a, b, (contract, ((), ())), preferred_element_type=F32)


def spread_kernel(q_ref, k_ref, v_ref, slot_ref, pos_ref, grad_ref, low_ref, dq_ref, dkv_ref,
           xa0, xa12, slots, gslab, onehot, zs, rs, zr, rr, place, kv, acc, dqs, hs, hr, ps, pr,
           outs, sem_as, sem_ar, sem_zs, sem_zr, sem_es, sem_er):
    dp = lax.axis_index("dp")
    me = lax.axis_index("ctx")
    z = me // PLANE
    j = me % PLANE
    x = j // 2
    c = j % 2
    other = j + 1 - 2 * c
    up = (z + 1) % NZ
    down = (z + NZ - 1) % NZ

    xa0[:, LOAD:, :] = jnp.zeros((PLANE, LOAD_PAD - LOAD, 256), BF16)
    xa12[:, LOAD:, :] = jnp.zeros((PLANE, LOAD_PAD - LOAD, 256), BF16)

    barrier = pltpu.get_barrier_semaphore()
    peers = [(z, (j + d) % PLANE) for d in range(1, PLANE)]
    peers += [((z + d) % NZ, j) for d in range(1, NZ)]
    peers += [(up, other), (down, other)]
    for pz, pj in peers:
        pl.semaphore_signal(barrier, inc=1, device_id=(dp, pz * PLANE + pj), device_id_type=MESH)
    pl.semaphore_wait(barrier, len(peers))

    def remote(src, dst, send, recv, pz, pj):
        pltpu.make_async_remote_copy(
            src_ref=src, dst_ref=dst, send_sem=send, recv_sem=recv,
            device_id=(dp, pz * PLANE + pj), device_id_type=MESH).start()

    def local(src, dst, sem):
        pltpu.make_async_copy(src, dst, sem).start()

    def await_bytes(ref, sem):
        pltpu.make_async_copy(ref, ref, sem).wait()

    rows = pl.ds(0, LOAD)

    def kv_dst():
        return xa0.at[j, rows, pl.ds(0, 128)]

    def pos_dst():
        return xa0.at[j, rows, pl.ds(128, 128)]

    def slot_dst():
        return slots.at[j]

    def q_dst():
        return xa12.at[j, rows, :]

    def grad_dst():
        return gslab.at[pl.ds(pl.multiple_of(j * TOK, TOK), TOK), :]

    def kv_column(pj):
        return pl.ds(pl.multiple_of((pj // 2) * 128, 128), 128)

    def wide_column(pj):
        return pl.ds(pl.multiple_of(pj * 256, 128), 256)

    for d in range(1, PLANE):
        pj = (j + d) % PLANE
        remote(slot_ref, slot_dst(), sem_as.at[0], sem_ar.at[0], z, pj)

        @pl.when(pj % 2 == 0)
        def _():
            remote(k_ref.at[:, kv_column(pj)], kv_dst(), sem_as.at[1], sem_ar.at[1], z, pj)

        @pl.when(pj % 2 == 1)
        def _():
            remote(v_ref.at[:, kv_column(pj)], kv_dst(), sem_as.at[1], sem_ar.at[1], z, pj)

        remote(pos_ref, pos_dst(), sem_as.at[2], sem_ar.at[2], z, pj)
    local(slot_ref, slot_dst(), sem_ar.at[0])

    @pl.when(c == 0)
    def _():
        local(k_ref.at[:, kv_column(j)], kv_dst(), sem_ar.at[1])

    @pl.when(c == 1)
    def _():
        local(v_ref.at[:, kv_column(j)], kv_dst(), sem_ar.at[1])

    local(pos_ref, pos_dst(), sem_ar.at[2])
    for d in range(1, PLANE):
        pj = (j + d) % PLANE
        remote(q_ref.at[:, wide_column(pj)], q_dst(), sem_as.at[3], sem_ar.at[3], z, pj)
    local(q_ref.at[:, wide_column(j)], q_dst(), sem_ar.at[3])
    for d in range(1, PLANE):
        pj = (j + d) % PLANE
        remote(grad_ref.at[:, wide_column(pj)], grad_dst(), sem_as.at[4], sem_ar.at[4], z, pj)
    local(grad_ref.at[:, wide_column(j)], grad_dst(), sem_ar.at[4])

    acc[...] = jnp.zeros_like(acc)

    def plane_of(d):
        return (z + ((d + 1) // 2) * (2 * (d % 2) - 1) + NZ) % NZ

    await_bytes(slots, sem_ar.at[0])
    await_bytes(xa0.at[:, rows, pl.ds(0, 128)], sem_ar.at[1])
    await_bytes(xa0.at[:, rows, pl.ds(128, 128)], sem_ar.at[2])

    def pack_first(zp):
        row = lax.broadcasted_iota(jnp.int32, (128, 4 * LOAD_PAD), 0) + zp * 128
        for quad in range(2):
            wanted = jnp.concatenate([slots[quad * 4 + i, 0:1, :] for i in range(4)], axis=1)
            hot = jnp.where(row == wanted, 1.0, 0.0).astype(BF16)
            onehot[zp, quad] = hot
            block = xa0[quad * 4:quad * 4 + 4].reshape(4 * LOAD_PAD, 256)
            packed = dot(hot, block)
            zs[0, zp, :, quad] = packed[:, :128].astype(BF16).reshape(PLANE, 16, 128)
            rs[zp, quad] = jnp.sum(packed[:, 128:].reshape(PLANE, 16, 128), axis=0).astype(BF16)

    @pl.loop(1, NZ)
    def _(d):
        zp = plane_of(d)
        pack_first(zp)
        remote(zs.at[0, zp], zr.at[0, :, :, z], sem_zs.at[0], sem_zr.at[0], zp, j)
        remote(rs.at[zp], rr.at[:, z], sem_zs.at[1], sem_zr.at[1], zp, j)

    pack_first(z)
    local(zs.at[0, z], zr.at[0, :, :, z], sem_zr.at[0])
    local(rs.at[z], rr.at[:, z], sem_zr.at[1])

    await_bytes(xa12.at[:, rows, :], sem_ar.at[3])

    def pack_second(zp):
        for quad in range(2):
            block = xa12[quad * 4:quad * 4 + 4].reshape(4 * LOAD_PAD, 256)
            packed = dot(onehot[zp, quad], block).astype(BF16)
            zs[1, zp, :, quad] = packed[:, :128].reshape(PLANE, 16, 128)
            zs[2, zp, :, quad] = packed[:, 128:].reshape(PLANE, 16, 128)

    @pl.loop(1, NZ)
    def _(d):
        zp = plane_of(d)
        pack_second(zp)
        remote(zs.at[1, zp], zr.at[1, :, :, z], sem_zs.at[2], sem_zr.at[2], zp, j)

    pack_second(z)
    local(zs.at[1, z], zr.at[1, :, :, z], sem_zr.at[2])

    await_bytes(rr, sem_zr.at[1])
    marks = [jnp.transpose(rr[quad].reshape(NZ * 16, 128).astype(F32)) for quad in range(2)]
    spot = lax.broadcasted_iota(jnp.int32, (TOK, 2 * NZ * 16), 0).astype(F32) + 1.0
    for o in range(PLANE):
        mark = jnp.concatenate([marks[0][o:o + 1], marks[1][o:o + 1]], axis=1)
        place[o] = jnp.where(spot == mark, 1.0, 0.0).astype(BF16)

    def settle(chunk, o):
        return dot(place[o], zr[chunk, o].reshape(2 * NZ * 16, 128)).astype(BF16)

    await_bytes(zr.at[0], sem_zr.at[0])

    @pl.loop(0, PLANE)
    def _(o):
        kv[c, pl.ds(pl.multiple_of(HALO + o * TOK, TOK), TOK), :] = settle(0, o)

    own_kv = kv.at[c, pl.ds(HALO, SLAB), :]
    remote(own_kv, own_kv, sem_es.at[0], sem_er.at[0], z, other)
    tail = kv.at[c, pl.ds(SLAB, HALO), :]
    head = kv.at[c, pl.ds(0, HALO), :]
    remote(tail, head, sem_es.at[1], sem_er.at[1], up, j)
    remote(tail, head, sem_es.at[1], sem_er.at[1], up, other)

    for part in range(4):
        pair = pl.ds(2 * part, 2)

        @pl.loop(1, NZ)
        def _(d):
            zp = plane_of(d)
            remote(zs.at[2, zp, pair], zr.at[2, pair, :, z], sem_zs.at[3], sem_zr.at[3 + part], zp, j)

        local(zs.at[2, z, pair], zr.at[2, pair, :, z], sem_zr.at[3 + part])

    await_bytes(own_kv, sem_er.at[0])
    await_bytes(kv.at[:, pl.ds(0, HALO), :], sem_er.at[1])
    await_bytes(gslab, sem_ar.at[4])

    def attend(head_index, b):
        window = pl.ds(pl.multiple_of(b * TOK, TOK), HALO + TOK)
        query = settle(1 + head_index, b)
        grad = gslab[pl.ds(pl.multiple_of(b * TOK, TOK), TOK), head_index * 128:head_index * 128 + 128]
        keys = kv[0, window, :]
        values = kv[1, window, :]
        key_index = lax.broadcasted_iota(jnp.int32, (HALO + TOK, TOK), 0)
        query_index = lax.broadcasted_iota(jnp.int32, (HALO + TOK, TOK), 1)
        allowed = (key_index >= low_ref[b]) & (key_index <= query_index + HALO)
        score = dot(keys, query, ((1,), (1,)))
        score = jnp.where(allowed, score, MASKED)
        top = jnp.max(score, axis=0, keepdims=True)
        weights = jnp.exp((score - top) * SCALE)
        weights = weights * (1.0 / jnp.sum(weights, axis=0, keepdims=True))
        grad_weights = dot(values, grad, ((1,), (1,)))
        row_dot = jnp.sum(weights * grad_weights, axis=0, keepdims=True)
        grad_score = (weights * (grad_weights - row_dot)).astype(BF16)
        acc[1, window, :] += dot(weights.astype(BF16), grad)
        acc[0, window, :] += dot(grad_score, query) * SCALE
        dqs[head_index, b] = (dot(grad_score, keys, ((0,), (0,))) * SCALE).astype(BF16)
        column = pl.ds(pl.multiple_of(j * 256 + head_index * 128, 128), 128)

        @pl.when(b == j)
        def _():
            local(dqs.at[head_index, b], dq_ref.at[:, column], sem_er.at[2])

        @pl.when(b != j)
        def _():
            remote(dqs.at[head_index, b], dq_ref.at[:, column], sem_es.at[2], sem_er.at[2], z, b)

    await_bytes(zr.at[1], sem_zr.at[2])

    @pl.loop(0, PLANE)
    def _(b):
        attend(0, b)

    for part in range(4):
        await_bytes(zr.at[2, pl.ds(2 * part, 2)], sem_zr.at[3 + part])

        @pl.loop(2 * part, 2 * part + 2)
        def _(b):
            attend(1, b)

        if part == 0:
            hs[...] = acc[:, :HALO, :].astype(BF16)
            remote(hs, hr, sem_es.at[3], sem_er.at[3], down, j)

    await_bytes(hr, sem_er.at[3])
    acc[:, SLAB:, :] += hr[...].astype(F32)
    ps[...] = acc[1 - c, HALO:, :].astype(BF16)
    remote(ps, pr, sem_es.at[4], sem_er.at[4], z, other)
    await_bytes(pr, sem_er.at[4])
    outs[...] = (acc[c, HALO:, :] + pr[...].astype(F32)).astype(BF16).reshape(PLANE, TOK, 128)
    column = pl.ds(pl.multiple_of(x * 128, 128), 128)
    for d in range(1, PLANE):
        pj = (j + d) % PLANE
        remote(outs.at[pj], dkv_ref.at[c, :, column], sem_es.at[5], sem_er.at[5], z, pj)
    local(outs.at[j], dkv_ref.at[c, :, column], sem_er.at[5])

    seven = pl.ds(0, PLANE - 1)
    await_bytes(dkv_ref, sem_er.at[5])
    await_bytes(dq_ref, sem_er.at[2])
    await_bytes(slots.at[seven], sem_as.at[0])
    await_bytes(xa0.at[seven, rows, pl.ds(0, 128)], sem_as.at[1])
    await_bytes(xa0.at[seven, rows, pl.ds(128, 128)], sem_as.at[2])
    await_bytes(xa12.at[seven, rows, :], sem_as.at[3])
    await_bytes(gslab.at[pl.ds(0, 7 * TOK), :], sem_as.at[4])
    most = pl.ds(0, NZ - 1)
    await_bytes(zs.at[0, most], sem_zs.at[0])
    await_bytes(rs.at[most], sem_zs.at[1])
    await_bytes(zs.at[1, most], sem_zs.at[2])
    await_bytes(zs.at[2, most], sem_zs.at[3])
    await_bytes(own_kv, sem_es.at[0])
    await_bytes(kv.at[:, pl.ds(0, HALO), :], sem_es.at[1])
    await_bytes(dqs.at[:, seven], sem_es.at[2])
    await_bytes(hs, sem_es.at[3])
    await_bytes(ps, sem_es.at[4])
    await_bytes(outs.at[seven], sem_es.at[5])


def mixed_kernel(q_ref, k_ref, v_ref, grad_ref, slab_ref, len_ref, dq_ref, dk_ref, dv_ref, flag_ref,
                 low, raw_kv, raw_q, sort_kv, sort_q, meta_out, meta_in, xk, xq, srow, info, gslab,
                 onehot, zs, ms, zr, mr, drow, spread, whole, ys, yr, ym_out, ym_in, place, kv, acc,
                 dqs, hs, hr, ps, pr, outs, sem_in, sem_as, sem_ar, sem_zs, sem_zr, sem_ys, sem_yr,
                 sem_es, sem_er, sem_pr):
    dp = lax.axis_index("dp")
    me = lax.axis_index("ctx")
    z = me // PLANE
    j = me % PLANE
    x = j // 2
    c = j % 2
    other = j + 1 - 2 * c
    up = (z + 1) % NZ
    down = (z + NZ - 1) % NZ

    barrier = pltpu.get_barrier_semaphore()
    plane = [((dp + e) % NDP, (j + d) % PLANE) for e in range(NDP) for d in range(PLANE)]
    peers = [(py, z, pj) for py, pj in plane[1:]]
    peers += [(dp, (z + d) % NZ, j) for d in range(1, NZ)]
    peers += [(dp, up, other), (dp, down, other)]
    for py, pz, pj in peers:
        pl.semaphore_signal(barrier, inc=1, device_id=(py, pz * PLANE + pj), device_id_type=MESH)

    def remote(src, dst, send, recv, pz, pj, py=dp):
        pltpu.make_async_remote_copy(
            src_ref=src, dst_ref=dst, send_sem=send, recv_sem=recv,
            device_id=(py, pz * PLANE + pj), device_id_type=MESH).start()

    def local(src, dst, sem):
        pltpu.make_async_copy(src, dst, sem).start()

    def await_bytes(ref, sem):
        pltpu.make_async_copy(ref, ref, sem).wait()

    rows = pl.ds(0, LOAD)
    key_lanes = pl.ds(0, 512)
    value_lanes = pl.ds(512, 512)
    local(k_ref, raw_kv.at[rows, key_lanes], sem_in.at[0])
    local(v_ref, raw_kv.at[rows, value_lanes], sem_in.at[1])
    local(q_ref, raw_q.at[rows, :], sem_in.at[2])

    raw_kv[LOAD:, :] = jnp.zeros((LOAD_PAD - LOAD, 1024), BF16)
    raw_q[LOAD:, :] = jnp.zeros((LOAD_PAD - LOAD, 2048), BF16)
    slab = slab_ref[0:1, :]
    kept = slab >= 0
    owner_f = jnp.where(kept, (slab >> 8) & (NZ * PLANE - 1), -1).astype(F32)
    mark_f = jnp.where(kept, (slab & (TOK - 1)) + 1, 0).astype(F32)
    lane = lax.broadcasted_iota(jnp.int32, (128, LOAD_PAD), 1)
    line = lax.broadcasted_iota(jnp.int32, (128, LOAD_PAD), 0)
    rank = jnp.zeros((1, LOAD_PAD), F32)
    less = jnp.zeros((1, LOAD_PAD), F32)
    for k in range(3):
        tile = slice(128 * k, 128 * k + 128)
        owner_col = jnp.transpose(jnp.broadcast_to(owner_f[:, tile], (LOAD_PAD, 128)))
        same = (owner_col == owner_f) & (line + 128 * k < lane)
        under = (owner_col < owner_f) & (owner_col >= 0.0)
        rank = rank + jnp.sum(jnp.where(same, 1.0, 0.0), axis=0, keepdims=True)
        less = less + jnp.sum(jnp.where(under, 1.0, 0.0), axis=0, keepdims=True)
    seat = jnp.where(kept, rank * 64.0 + less * 0.25, -1.0)
    line_f = line.astype(F32)
    halves = [jnp.where(line_f + 128.0 * h == seat, 1.0, 0.0).astype(BF16) for h in range(2)]
    sorter = jnp.concatenate(halves, axis=0)
    sub = lax.broadcasted_iota(jnp.int32, (8, LOAD_PAD), 0)
    facts = jnp.where(sub == 0, owner_f, jnp.where(sub == 1, mark_f, 0.0)).astype(BF16)
    for quarter in range(NDP):
        chosen = (line_f + 64.0 * quarter == seat) & (line < 64)
        picked = jnp.where(chosen, 1.0, 0.0).astype(BF16)
        meta_out[quarter] = dot(facts, picked, ((1,), (1,)))

    await_bytes(raw_kv.at[rows, key_lanes], sem_in.at[0])
    await_bytes(raw_kv.at[rows, value_lanes], sem_in.at[1])
    for half in range(2):
        moved = dot(sorter, raw_kv[:, half * 512:half * 512 + 512]).astype(BF16)
        for head in range(KV_HEADS):
            piece = moved[:, head * 128:head * 128 + 128]
            sort_kv[:, 2 * head + half] = piece.reshape(NDP, 64, 128)

    pl.semaphore_wait(barrier, len(peers))

    here = dp * PLANE + j
    for py, pj in plane[1:]:
        remote(meta_out.at[py], meta_in.at[here], sem_as.at[0], sem_ar.at[0], z, pj, py)
        remote(sort_kv.at[py, pj], xk.at[here], sem_as.at[1], sem_ar.at[1], z, pj, py)
    local(meta_out.at[dp], meta_in.at[here], sem_ar.at[0])
    local(sort_kv.at[dp, j], xk.at[here], sem_ar.at[1])

    await_bytes(raw_q.at[rows, :], sem_in.at[2])
    for jj in range(PLANE):
        moved = dot(sorter, raw_q[:, jj * 256:jj * 256 + 256]).astype(BF16)
        sort_q[:, jj] = moved.reshape(NDP, 64, 256)
    for py, pj in plane[1:]:
        remote(sort_q.at[py, pj], xq.at[here], sem_as.at[2], sem_ar.at[2], z, pj, py)
    local(sort_q.at[dp, j], xq.at[here], sem_ar.at[2])

    def grad_dst():
        return gslab.at[pl.ds(pl.multiple_of(j * TOK, TOK), TOK), :]

    def wide_column(pj):
        return pl.ds(pl.multiple_of(pj * 256, 128), 256)

    for d in range(1, PLANE):
        pj = (j + d) % PLANE
        remote(grad_ref.at[:, wide_column(pj)], grad_dst(), sem_as.at[3], sem_ar.at[3], z, pj)
    local(grad_ref.at[:, wide_column(j)], grad_dst(), sem_ar.at[3])

    def step_of(d):
        return ((d + 1) // 2) * (2 * (d % 2) - 1)

    def plane_of(d):
        return (z + step_of(d) + NZ) % NZ

    def source_of(d):
        return (z - step_of(d) + NZ) % NZ

    await_bytes(meta_in, sem_ar.at[0])
    sources = NDP * PLANE
    owners = meta_in[:, 0, :]
    marks = meta_in[:, 1, :]
    lane = lax.broadcasted_iota(jnp.int32, (sources, 128), 1)
    source = lax.broadcasted_iota(jnp.int32, (sources, 128), 0)
    used = lane < 64
    owner_i = owners.astype(jnp.int32)
    toward = jnp.where(used, owner_i >> 3, -1)
    counts = jnp.zeros((sources, 128), F32)
    for zz in range(NZ):
        count = jnp.sum(jnp.where(toward == zz, 1.0, 0.0), axis=1, keepdims=True)
        counts = jnp.where(lane == zz, count, counts)
    earlier = jnp.where(
        lax.broadcasted_iota(jnp.int32, (sources, sources), 1)
        < lax.broadcasted_iota(jnp.int32, (sources, sources), 0), 1.0, 0.0).astype(BF16)
    base = dot(earlier, counts.astype(BF16))
    passed = jnp.zeros((sources, 1), F32)
    lane_f = lane.astype(F32)
    slot = jnp.full((sources, 128), -1.0, F32)
    for zz in range(NZ):
        order = lane_f + (base[:, zz:zz + 1] - passed)
        passed = passed + counts[:, zz:zz + 1]
        slot = jnp.where((toward == zz) & (order < CAP), order + zz * CAP, slot)
    overflow = jnp.max(jnp.sum(counts, axis=0, keepdims=True), axis=1, keepdims=True)
    overflow = jnp.where(overflow > CAP, 1.0, 0.0)
    kind = ((source >> 3) * PLANE + (owner_i & (PLANE - 1))).astype(F32)

    def paired(value):
        turned = pltpu.roll(value, 64, 1)
        first = lax.broadcasted_iota(jnp.int32, (1, 128), 1) < 64
        return jnp.concatenate(
            [jnp.where(first, value[2 * p:2 * p + 1], turned[2 * p + 1:2 * p + 2])
             for p in range(sources // 2)], axis=1)

    srow[...] = jnp.broadcast_to(paired(slot), (8, SLAB))
    sub = lax.broadcasted_iota(jnp.int32, (8, SLAB), 0)
    info[...] = jnp.where(sub == 0, paired(kind), jnp.where(sub == 1, paired(marks), 1.0)).astype(BF16)

    await_bytes(xk, sem_ar.at[1])

    def pack_first(zp):
        row = (lax.broadcasted_iota(jnp.int32, (CAP, SLAB), 0) + zp * CAP).astype(F32)
        hot = jnp.where(row == srow[0:1, :], 1.0, 0.0).astype(BF16)
        onehot[zp] = hot
        zs[0, zp] = dot(hot, xk[...].reshape(SLAB, 128)).astype(BF16)

    landed = pl.ds(0, CAP)

    @pl.loop(1, NZ)
    def _(d):
        zp = plane_of(d)
        pack_first(zp)
        remote(zs.at[0, zp], zr.at[0, z, landed, :], sem_zs.at[0], sem_zr.at[0], zp, j)

    pack_first(z)
    local(zs.at[0, z], zr.at[0, z, landed, :], sem_zr.at[0])

    zr[:, :, CAP:, :] = jnp.zeros((3, NZ, 256 - CAP, 128), BF16)
    sub8 = lax.broadcasted_iota(jnp.int32, (8, CAP), 0)

    @pl.loop(0, NZ)
    def _(d):
        zp = plane_of(d)
        ms[zp] = jnp.zeros((8, 256), F32)
        told = dot(info[...], onehot[zp], ((1,), (1,)))
        ms[zp, :, 0:CAP] = jnp.where(sub8 == 7, overflow, told)

    for d in range(1, NZ):
        zp = plane_of(d)
        remote(ms.at[zp], mr.at[z], sem_zs.at[1], sem_zr.at[1], zp, j)
    local(ms.at[z], mr.at[z], sem_zr.at[1])

    await_bytes(xq, sem_ar.at[2])

    @pl.loop(0, NZ)
    def _(d):
        zp = plane_of(d)
        packed = dot(onehot[zp], xq[...].reshape(SLAB, 256))
        zs[1, zp] = packed[:, :128].astype(BF16)
        zs[2, zp] = packed[:, 128:].astype(BF16)

    for d in range(1, NZ):
        zp = plane_of(d)
        remote(zs.at[1, zp], zr.at[1, z, landed, :], sem_zs.at[2], sem_zr.at[2], zp, j)
    local(zs.at[1, z], zr.at[1, z, landed, :], sem_zr.at[2])

    lengths = jnp.broadcast_to(len_ref[...].astype(F32), (DOCS, DOCS))
    doc_row = lax.broadcasted_iota(jnp.int32, (DOCS, DOCS), 0)
    doc_col = lax.broadcasted_iota(jnp.int32, (DOCS, DOCS), 1)
    doc_ends = jnp.sum(jnp.where(doc_col <= doc_row, lengths, 0.0), axis=1, keepdims=True)
    doc_size = jnp.sum(jnp.where(doc_col == doc_row, lengths, 0.0), axis=1, keepdims=True)
    offset = lax.broadcasted_iota(jnp.int32, (1, TOK), 1)
    for b in range(PLANE):
        place_at = (offset + (z * SLAB + b * TOK)).astype(F32)
        start = jnp.sum(jnp.where(doc_ends <= place_at, doc_size, 0.0), axis=0, keepdims=True)
        low[b] = start.astype(jnp.int32) - (z * SLAB + b * TOK - HALO)
    acc[...] = jnp.zeros_like(acc)

    await_bytes(mr, sem_zr.at[1])
    flag = mr[0, 7:8, 0:128]
    for zz in range(1, NZ):
        flag = jnp.maximum(flag, mr[zz, 7:8, 0:128])
    flag_ref[...] = jnp.broadcast_to(flag, (8, 128)).astype(jnp.int32)
    upper = jnp.where(
        lax.broadcasted_iota(jnp.int32, (256, 256), 0)
        < lax.broadcasted_iota(jnp.int32, (256, 256), 1), 1.0, 0.0).astype(BF16)
    class_id = lax.broadcasted_iota(jnp.int32, (sources, 256), 0).astype(F32)
    seen = jnp.zeros((sources, 1), F32)
    for zz in range(NZ):
        valid = mr[zz, 2:3, :] > 0.5
        mine = (class_id == mr[zz, 0:1, :]) & valid
        mine_f = jnp.where(mine, 1.0, 0.0)
        order = dot(mine_f.astype(BF16), upper) + seen
        seen = seen + jnp.sum(mine_f, axis=1, keepdims=True)
        spot = jnp.sum(jnp.where(mine, order + class_id * 64.0, 0.0), axis=0, keepdims=True)
        drow[zz] = jnp.broadcast_to(jnp.where(valid, spot, -1.0), (8, 256))
    whole[...] = jnp.zeros_like(whole)

    @pl.loop(0, NDP)
    def _(w):
        line = (lax.broadcasted_iota(jnp.int32, (512, 256), 0) + w * 512).astype(F32)
        total = jnp.zeros((8, 512), F32)
        for zz in range(NZ):
            hot = jnp.where(line == drow[zz, 0:1, :], 1.0, 0.0).astype(BF16)
            spread[zz, pl.ds(pl.multiple_of(w * 512, 512), 512), :] = hot
            total = total + dot(mr[zz].astype(BF16), hot, ((1,), (1,)))
        ym_out[w] = total

    for e in range(1, NDP):
        w = (dp + e) % NDP
        remote(ym_out.at[w], ym_in.at[dp], sem_ys.at[0], sem_yr.at[0], z, j, w)
    local(ym_out.at[dp], ym_in.at[dp], sem_yr.at[0])

    def gather_all(chunk):
        @pl.loop(0, NDP)
        def _(w):
            block = pl.ds(pl.multiple_of(w * 512, 512), 512)
            total = jnp.zeros((512, 128), F32)
            for zz in range(NZ):
                total = total + dot(spread[zz, block, :], zr[chunk, zz])
            ys[chunk, w] = total.astype(BF16).reshape(PLANE, 64, 128)

    def send_back(chunk):
        for e in range(1, NDP):
            w = (dp + e) % NDP
            remote(ys.at[chunk, w], yr.at[chunk, :, dp], sem_ys.at[1 + chunk], sem_yr.at[1 + chunk], z, j, w)
        local(ys.at[chunk, dp], yr.at[chunk, :, dp], sem_yr.at[1 + chunk])

    await_bytes(zr.at[0, :, landed, :], sem_zr.at[0])
    gather_all(0)
    send_back(0)

    await_bytes(ym_in, sem_yr.at[0])
    first = lax.broadcasted_iota(jnp.int32, (1, 128), 1) < 64
    point = lax.broadcasted_iota(jnp.int32, (TOK, TOK), 0).astype(F32) + 1.0
    for o in range(PLANE):
        tile = slice(128 * (o // 2), 128 * (o // 2) + 128)
        parts = [ym_in[e, 0:8, tile][1:2] for e in range(NDP)]
        turned = [pltpu.roll(ym_in[e, 0:8, tile], 64, 1)[1:2] for e in range(NDP)]
        left = parts if o % 2 == 0 else turned
        right = turned if o % 2 == 0 else parts
        mark = jnp.concatenate(
            [jnp.where(first, left[0], right[1]), jnp.where(first, left[2], right[3])], axis=1)
        place[o] = jnp.where(point == mark, 1.0, 0.0).astype(BF16)

    def settle(chunk, o):
        return dot(place[o], yr[chunk, o].reshape(TOK, 128)).astype(BF16)

    await_bytes(yr.at[0], sem_yr.at[1])

    @pl.loop(0, PLANE)
    def _(o):
        kv[c, pl.ds(pl.multiple_of(HALO + o * TOK, TOK), TOK), :] = settle(0, o)

    own_kv = kv.at[c, pl.ds(HALO, SLAB), :]
    remote(own_kv, own_kv, sem_es.at[0], sem_er.at[0], z, other)
    tail = kv.at[c, pl.ds(SLAB, HALO), :]
    head = kv.at[c, pl.ds(0, HALO), :]
    remote(tail, head, sem_es.at[1], sem_er.at[1], up, j)
    remote(tail, head, sem_es.at[1], sem_er.at[1], up, other)

    for d in range(NZ):
        zp = plane_of(d)
        if d == 0:
            local(zs.at[2, zp], zr.at[2, z, landed, :], sem_zr.at[3])
        else:
            remote(zs.at[2, zp], zr.at[2, z, landed, :], sem_zs.at[3], sem_zr.at[3 + d // 4], zp, j)

    await_bytes(own_kv, sem_er.at[0])
    await_bytes(kv.at[:, pl.ds(0, HALO), :], sem_er.at[1])
    await_bytes(gslab, sem_ar.at[3])

    def attend(head_index, b):
        start = b * TOK if isinstance(b, int) else pl.multiple_of(b * TOK, TOK)
        window = pl.ds(start, HALO + TOK)
        query = settle(1 + head_index, b)
        grad = gslab[pl.ds(start, TOK), head_index * 128:head_index * 128 + 128]
        keys = kv[0, window, :]
        values = kv[1, window, :]
        key_index = lax.broadcasted_iota(jnp.int32, (HALO + TOK, TOK), 0)
        query_index = lax.broadcasted_iota(jnp.int32, (HALO + TOK, TOK), 1)
        allowed = (key_index >= low[b]) & (key_index <= query_index + HALO)
        score = dot(keys, query, ((1,), (1,)))
        score = jnp.where(allowed, score, MASKED)
        top = jnp.max(score, axis=0, keepdims=True)
        weights = jnp.exp((score - top) * SCALE)
        weights = weights * (1.0 / jnp.sum(weights, axis=0, keepdims=True))
        grad_weights = dot(values, grad, ((1,), (1,)))
        row_dot = jnp.sum(weights * grad_weights, axis=0, keepdims=True)
        grad_score = (weights * (grad_weights - row_dot)).astype(BF16)
        acc[1, window, :] += dot(weights.astype(BF16), grad)
        acc[0, window, :] += dot(grad_score, query) * SCALE
        dqs[head_index, b] = (dot(grad_score, keys, ((0,), (0,))) * SCALE).astype(BF16)
        column = pl.ds(pl.multiple_of(j * 256 + head_index * 128, 128), 128)

        @pl.when(j == b)
        def _():
            local(dqs.at[head_index, b], dq_ref.at[:, column], sem_er.at[2])

        @pl.when(j != b)
        def _():
            remote(dqs.at[head_index, b], dq_ref.at[:, column], sem_es.at[2], sem_er.at[2], z, b)

    def hand_over(t):
        ps[t] = acc[1 - c, HALO + t * TOK:HALO + t * TOK + TOK, :].astype(BF16)
        remote(ps.at[t], pr.at[t], sem_es.at[4], sem_pr.at[t], z, other)

    def finish(t):
        await_bytes(pr.at[t], sem_pr.at[t])
        total = acc[c, HALO + t * TOK:HALO + t * TOK + TOK, :] + pr[t].astype(F32)
        outs[t] = total.astype(BF16)
        column = pl.ds(pl.multiple_of(x * 128, 128), 128)
        for which, ref in ((0, dk_ref), (1, dv_ref)):
            @pl.when((c == which) & (j == t))
            def _():
                local(outs.at[t], ref.at[:, column], sem_er.at[4 + which])

            @pl.when((c == which) & (j != t))
            def _():
                remote(outs.at[t], ref.at[:, column], sem_es.at[5], sem_er.at[4 + which], z, t)

    await_bytes(zr.at[1, :, landed, :], sem_zr.at[2])
    gather_all(1)
    send_back(1)
    await_bytes(yr.at[1], sem_yr.at[2])

    @pl.loop(0, PLANE)
    def _(b):
        attend(0, b)

    for group in range(4):
        await_bytes(zr.at[2, pl.ds(0, 4), landed, :], sem_zr.at[3 + group])

        @pl.loop(0, NDP)
        def _(w):
            block = pl.ds(pl.multiple_of(w * 512, 512), 512)
            total = whole[block, :]
            for d in range(4 * group, 4 * group + 4):
                zz = source_of(d)
                total = total + dot(spread[zz, block, :], zr[2, zz])
            if group < 3:
                whole[block, :] = total
            else:
                ys[2, w] = total.astype(BF16).reshape(PLANE, 64, 128)

    for part in range(4):
        pair = pl.ds(2 * part, 2)
        for e in range(1, NDP):
            w = (dp + e) % NDP
            remote(ys.at[2, w, pair], yr.at[2, pair, dp], sem_ys.at[3], sem_yr.at[3 + part], z, j, w)
        local(ys.at[2, dp, pair], yr.at[2, pair, dp], sem_yr.at[3 + part])

    for b in range(PLANE):
        if b == PLANE - 1:
            await_bytes(hr, sem_er.at[3])
            acc[:, SLAB:, :] += hr[...].astype(F32)
        if b % 2 == 0:
            await_bytes(yr.at[2, pl.ds(b, 2)], sem_yr.at[3 + b // 2])
        attend(1, b)
        if b == 1:
            hs[...] = acc[:, :HALO, :].astype(BF16)
            remote(hs, hr, sem_es.at[3], sem_er.at[3], down, j)
        if b >= 2:
            hand_over(b - 2)
        if b >= 3:
            finish(b - 3)
    hand_over(6)
    hand_over(7)
    for t in (5, 6, 7):
        finish(t)

    seven = pl.ds(0, PLANE - 1)
    most = pl.ds(0, NZ - 1)
    many = pl.ds(0, NDP * PLANE - 1)
    three = pl.ds(0, NDP - 1)
    await_bytes(meta_in.at[many], sem_as.at[0])
    await_bytes(xk.at[many], sem_as.at[1])
    await_bytes(xq.at[many], sem_as.at[2])
    await_bytes(gslab.at[pl.ds(0, 7 * TOK), :], sem_as.at[3])
    await_bytes(zs.at[0, most], sem_zs.at[0])
    await_bytes(ms.at[most], sem_zs.at[1])
    await_bytes(zs.at[1, most], sem_zs.at[2])
    await_bytes(zs.at[2, most], sem_zs.at[3])
    await_bytes(ym_out.at[three], sem_ys.at[0])
    for chunk in range(3):
        await_bytes(ys.at[chunk, three], sem_ys.at[1 + chunk])
    await_bytes(own_kv, sem_es.at[0])
    await_bytes(kv.at[:, pl.ds(0, HALO), :], sem_es.at[1])
    await_bytes(dqs.at[:, seven], sem_es.at[2])
    await_bytes(hs, sem_es.at[3])
    await_bytes(ps, sem_es.at[4])
    await_bytes(outs.at[seven], sem_es.at[5])
    await_bytes(dq_ref, sem_er.at[2])
    await_bytes(dk_ref, sem_er.at[4])
    await_bytes(dv_ref, sem_er.at[5])


OUT_SHAPES = (
    jax.ShapeDtypeStruct((TOK, HEADS * HEAD_DIM), BF16),
    jax.ShapeDtypeStruct((TOK, KV_HEADS * HEAD_DIM), BF16),
    jax.ShapeDtypeStruct((TOK, KV_HEADS * HEAD_DIM), BF16),
)


def spread_call(queries, key_rows, value_rows, slab_row, doc_lengths, out_grad):
    me = lax.axis_index("ctx")
    z = me // PLANE
    j = me % PLANE
    kept = slab_row >= 0
    owner = jnp.where(kept, slab_row // TOK % (NZ * PLANE), -1)
    order = jnp.arange(LOAD, dtype=jnp.int32)
    earlier = (owner[:, None] == owner[None, :]) & (order[:, None] < order[None, :])
    rank = jnp.sum(earlier.astype(jnp.int32), axis=0)
    slot = jnp.where(kept, owner * 16 + (j % 4) * 4 + rank, -1)
    slot = jnp.pad(slot, (0, LOAD_PAD - LOAD), constant_values=-1)
    slot = jnp.broadcast_to(slot[None, :], (8, LOAD_PAD))
    lane = jnp.arange(128, dtype=jnp.int32)
    mark = jnp.where(kept, slab_row % TOK + 1, 0)
    pos = jnp.where(lane[None, :] == (owner % PLANE)[:, None], mark[:, None], 0).astype(BF16)
    lengths = doc_lengths[0]
    doc_ends = jnp.cumsum(lengths)
    position = z * SLAB + jnp.arange(SLAB, dtype=jnp.int32)
    doc_start = jnp.sum(
        jnp.where(doc_ends[:, None] <= position[None, :], lengths[:, None], 0), axis=0
    ).reshape(PLANE, 1, TOK)
    base = z * SLAB + jnp.arange(PLANE, dtype=jnp.int32) * TOK - HALO
    low = doc_start - base[:, None, None]
    any_spec = pl.BlockSpec(memory_space=pl.ANY)
    vmem_spec = pl.BlockSpec(memory_space=pltpu.VMEM)
    dq, dkv = pl.pallas_call(
        spread_kernel,
        out_shape=(
            jax.ShapeDtypeStruct((TOK, HEADS * HEAD_DIM), BF16),
            jax.ShapeDtypeStruct((2, TOK, KV_HEADS * HEAD_DIM), BF16),
        ),
        in_specs=[any_spec] * 6 + [vmem_spec],
        out_specs=(any_spec, any_spec),
        scratch_shapes=[
            pltpu.VMEM((PLANE, LOAD_PAD, 256), BF16),
            pltpu.VMEM((PLANE, LOAD_PAD, 256), BF16),
            pltpu.VMEM((PLANE, 8, LOAD_PAD), jnp.int32),
            pltpu.VMEM((SLAB, 256), BF16),
            pltpu.VMEM((NZ, 2, 128, 4 * LOAD_PAD), BF16),
            pltpu.VMEM((3, NZ, PLANE, 2, 16, 128), BF16),
            pltpu.VMEM((NZ, 2, 16, 128), BF16),
            pltpu.VMEM((3, PLANE, 2, NZ, 16, 128), BF16),
            pltpu.VMEM((2, NZ, 16, 128), BF16),
            pltpu.VMEM((PLANE, TOK, 2 * NZ * 16), BF16),
            pltpu.VMEM((2, HALO + SLAB, 128), BF16),
            pltpu.VMEM((2, HALO + SLAB, 128), F32),
            pltpu.VMEM((2, PLANE, TOK, 128), BF16),
            pltpu.VMEM((2, HALO, 128), BF16),
            pltpu.VMEM((2, HALO, 128), BF16),
            pltpu.VMEM((SLAB, 128), BF16),
            pltpu.VMEM((SLAB, 128), BF16),
            pltpu.VMEM((PLANE, TOK, 128), BF16),
            pltpu.SemaphoreType.DMA((5,)),
            pltpu.SemaphoreType.DMA((5,)),
            pltpu.SemaphoreType.DMA((4,)),
            pltpu.SemaphoreType.DMA((7,)),
            pltpu.SemaphoreType.DMA((6,)),
            pltpu.SemaphoreType.DMA((6,)),
        ],
        compiler_params=pltpu.CompilerParams(
            collective_id=1, has_side_effects=True, vmem_limit_bytes=60 * 1024 * 1024
        ),
        name="spread_attention",
    )(queries, key_rows, value_rows, slot, pos, out_grad, low)
    return (dq, dkv[0], dkv[1])


def mixed_call(queries, key_rows, value_rows, out_grad, slab, doc_lengths):
    any_spec = pl.BlockSpec(memory_space=pl.ANY)
    vmem_spec = pl.BlockSpec(memory_space=pltpu.VMEM)
    dma = pltpu.SemaphoreType.DMA
    return pl.pallas_call(
        mixed_kernel,
        out_shape=OUT_SHAPES + (jax.ShapeDtypeStruct((8, 128), jnp.int32),),
        in_specs=[any_spec] * 4 + [vmem_spec] * 2,
        out_specs=(any_spec, any_spec, any_spec, vmem_spec),
        scratch_shapes=[
            pltpu.VMEM((PLANE, 1, TOK), jnp.int32),
            pltpu.VMEM((LOAD_PAD, 1024), BF16),
            pltpu.VMEM((LOAD_PAD, 2048), BF16),
            pltpu.VMEM((NDP, PLANE, 64, 128), BF16),
            pltpu.VMEM((NDP, PLANE, 64, 256), BF16),
            pltpu.VMEM((NDP, 8, 128), F32),
            pltpu.VMEM((NDP * PLANE, 8, 128), F32),
            pltpu.VMEM((NDP * PLANE, 64, 128), BF16),
            pltpu.VMEM((NDP * PLANE, 64, 256), BF16),
            pltpu.VMEM((8, SLAB), F32),
            pltpu.VMEM((8, SLAB), BF16),
            pltpu.VMEM((SLAB, 256), BF16),
            pltpu.VMEM((NZ, CAP, SLAB), BF16),
            pltpu.VMEM((3, NZ, CAP, 128), BF16),
            pltpu.VMEM((NZ, 8, 256), F32),
            pltpu.VMEM((3, NZ, 256, 128), BF16),
            pltpu.VMEM((NZ, 8, 256), F32),
            pltpu.VMEM((NZ, 8, 256), F32),
            pltpu.VMEM((NZ, SLAB, 256), BF16),
            pltpu.VMEM((SLAB, 128), F32),
            pltpu.VMEM((3, NDP, PLANE, 64, 128), BF16),
            pltpu.VMEM((3, PLANE, NDP, 64, 128), BF16),
            pltpu.VMEM((NDP, 8, 512), F32),
            pltpu.VMEM((NDP, 8, 512), F32),
            pltpu.VMEM((PLANE, TOK, TOK), BF16),
            pltpu.VMEM((2, HALO + SLAB, 128), BF16),
            pltpu.VMEM((2, HALO + SLAB, 128), F32),
            pltpu.VMEM((2, PLANE, TOK, 128), BF16),
            pltpu.VMEM((2, HALO, 128), BF16),
            pltpu.VMEM((2, HALO, 128), BF16),
            pltpu.VMEM((PLANE, TOK, 128), BF16),
            pltpu.VMEM((PLANE, TOK, 128), BF16),
            pltpu.VMEM((PLANE, TOK, 128), BF16),
            dma((3,)), dma((4,)), dma((4,)), dma((4,)), dma((7,)), dma((4,)), dma((7,)),
            dma((6,)), dma((6,)), dma((8,)),
        ],
        compiler_params=pltpu.CompilerParams(
            collective_id=0, has_side_effects=True, vmem_limit_bytes=62 * 1024 * 1024
        ),
        name="mixed_attention",
    )(queries, key_rows, value_rows, out_grad, slab, doc_lengths)


def body(queries, key_rows, value_rows, slab_row, doc_lengths, out_grad):
    slab = jnp.pad(slab_row, (0, LOAD_PAD - LOAD), constant_values=-1)
    slab = jnp.broadcast_to(slab[None, :], (8, LOAD_PAD))
    operands = (queries, key_rows, value_rows, slab_row, doc_lengths, out_grad)
    dq, dk, dv, flag = mixed_call(queries, key_rows, value_rows, out_grad, slab, doc_lengths)
    return lax.cond(flag[0, 0] > 0, lambda: tuple(spread_call(*operands)), lambda: (dq, dk, dv))


def solution(mesh):
    in_specs = (
        P(("dp", "ctx"), None),
        P(("dp", "ctx"), None),
        P(("dp", "ctx"), None),
        P(("dp", "ctx")),
        P("dp", None),
        P(("dp", "ctx"), None),
    )
    out_specs = (P(("dp", "ctx"), None), P(("dp", "ctx"), None), P(("dp", "ctx"), None))
    return jax.shard_map(body, mesh=mesh, in_specs=in_specs, out_specs=out_specs, check_vma=False)
```
